32 devices in a mesh: seq: 8 (over z, y), head: 4 (over x, core).
Axes of the slice: x: 2, y: 2, z: 4, core: 2. Of those that a mesh axis runs over, the one named last changes fastest.
Arguments:
- queries: bfloat16 [4096, 4096], P(('seq', 'head')), may hold values from -6 to 6
- keys: bfloat16 [4096, 2, 4096], P(('seq', 'head')), may hold values from -6 to 6
- values: bfloat16 [4096, 2, 4096], P(('seq', 'head')), may hold values from -6 to 6
- betas: bfloat16 [4096, 2, 16], P(('seq', 'head')), may hold values from 0.2 to 2, as said below
- gate: bfloat16 [4096, 4096], P(('seq', 'head')), may hold values from -6 to 6
- norm_gain: float32 [256], replicated, may hold values from 0.1 to 1.9
Outputs:
- mixed: bfloat16 [4096, 4096], P(('seq', 'head'))
The draws below stay inside these ranges and needn't reach their ends.
Inputs may be any that keep to these rules, and one draw needn't show every extreme that they name: `betas`: each entry is the step size of one reflection of one head.
All inputs are finite; a program needn't handle non-finite values.
Results may differ from the reference program's by a relative error of at most 0.0049.
Values may be sent and summed in bfloat16 or wider, within the bound.
No kernel may reach another device: no remote copies, remote signals or barrier semaphores. Data moves between devices by JAX's collectives and lax.ppermute only.
A program may use at most 128 MiB of HBM per device.

```python
import jax
import jax.numpy as jnp
from jax import lax

H = 16
DK = 256
REFL = 2
CT = 128
STREAM_LENGTH = 4096


def draw_betas(key, part):
    first_key, second_key, third_key, mirror_direction_last = jax.random.split(jax.random.fold_in(key, 17), 4)
    slow_share = 0.5
    slow_heads = jax.random.uniform(first_key, (H,)) < slow_share
    slow_forget_factors = jax.random.uniform(second_key, (STREAM_LENGTH, REFL, H), minval=1.996, maxval=2.0)
    quick_decay_rates = jax.random.uniform(third_key, (STREAM_LENGTH, REFL, H), minval=0.2, maxval=1.8)
    segment_groups = jax.random.uniform(mirror_direction_last, (STREAM_LENGTH, 1, 1)) < 8.0 / STREAM_LENGTH
    slow_payload_vectors = jnp.where(segment_groups, 1.0, slow_forget_factors)
    rates = jnp.where(slow_heads[None, None, :], slow_payload_vectors, quick_decay_rates)
    return rates.astype(jnp.bfloat16)


def level_of(rng, dims, cuts, low, high):
    gain = 1.0
    for dim, blocks in cuts:
        draws = jax.random.uniform(jax.random.fold_in(jax.random.fold_in(rng, 6), dim), (blocks,), jnp.float32, low / len(cuts), high / len(cuts))
        gain = gain * jnp.repeat(jnp.exp(draws), dims[dim] // blocks).reshape((-1,) + (1,) * (len(dims) - 1 - dim))
    return gain


def normal_values(stream_key, extent, spread, limit, cuts=(), kind=jnp.bfloat16):
    factor_of = level_of(stream_key, extent, cuts, -0.22, 0.18) if cuts else 1.0
    result = jax.random.normal(stream_key, extent, jnp.float32) * spread * factor_of
    return jnp.minimum(jnp.maximum(result, -limit), limit).astype(kind)


def setup_inputs(seed: int = 0) -> dict:
    arg_keys = jax.random.split(jax.random.key(seed), 7)
    queries = normal_values(arg_keys[0], (STREAM_LENGTH, H * DK), 1.0, 6.0, ((0, 32),))
    keys = normal_values(arg_keys[1], (STREAM_LENGTH, REFL, H * DK), 1.0, 6.0, ((0, 32),))
    values = normal_values(arg_keys[2], (STREAM_LENGTH, REFL, H * DK), 1.0, 6.0, ((0, 32),))
    betas = draw_betas(jax.random.fold_in(arg_keys[6], 71), 0)
    gate = normal_values(arg_keys[4], (STREAM_LENGTH, H * DK), 1.0, 6.0, ((0, 32),))
    norm_gain = jnp.clip(1.0 + 0.18 * jax.random.normal(arg_keys[5], (DK,), jnp.float32), 0.1, 1.9)
    return {"queries": queries, "keys": keys, "values": values, "betas": betas, "gate": gate, "norm_gain": norm_gain}


epsilon = 1e-06
highest = lax.Precision.HIGHEST

def unit_rows(matrix):
    return matrix / jnp.sqrt(lax.optimization_barrier(jnp.sum(matrix * matrix, axis=-1, keepdims=True)) + epsilon)

def block_mask(block_tokens, reflections):
    step_iota = lax.broadcasted_iota(jnp.int32, (block_tokens, block_tokens * reflections), 1)
    token_iota = lax.broadcasted_iota(jnp.int32, (block_tokens, block_tokens * reflections), 0)
    return step_iota // reflections <= token_iota

def head_pass(input_arrays):
    query_rows, key_rows, value_rows, beta_rows = input_arrays
    row_count = query_rows.shape[0]
    width_per_head = query_rows.shape[-1]
    blocks = row_count // CT
    block_steps = CT * REFL
    query_blocks = unit_rows(query_rows.astype(jnp.float32)).reshape(blocks, CT, width_per_head)
    k_blocks = unit_rows(key_rows.astype(jnp.float32)).reshape(blocks, block_steps, width_per_head)
    v_blocks = value_rows.astype(jnp.float32).reshape(blocks, block_steps, width_per_head)
    b_blocks = beta_rows.astype(jnp.float32).reshape(blocks, block_steps)
    causal = block_mask(CT, REFL)

    def advance(carried, pieces):
        q_now, k_now, v_now, b_now = pieces
        gram_rows = jnp.dot(k_now, k_now.T, precision=highest)
        lower_part = jnp.tril(gram_rows, -1) * b_now[None, :]
        solved = lax.linalg.triangular_solve(lower_part, jnp.concatenate([k_now, v_now], axis=1), left_side=True, lower=True, unit_diagonal=True)
        w_rows = solved[:, :width_per_head] * b_now[:, None]
        y_rows = solved[:, width_per_head:] * b_now[:, None]
        update_rows = y_rows - jnp.dot(w_rows, carried, precision=highest)
        scores = jnp.where(causal, jnp.dot(q_now, k_now.T, precision=highest), jnp.zeros((), jnp.float32))
        output = jnp.dot(q_now, carried, precision=highest) + jnp.dot(scores, update_rows, precision=highest)
        carried = carried + jnp.dot(k_now.T, update_rows, precision=highest)
        return (carried, output)
    start = jnp.zeros((width_per_head, width_per_head), jnp.float32)
    final_state, outputs = lax.scan(advance, start, (query_blocks, k_blocks, v_blocks, b_blocks))
    return outputs.reshape(row_count, width_per_head)

def reference(queries, keys, values, betas, gate, norm_gain):
    row_count = queries.shape[0]
    width_per_head = norm_gain.shape[0]
    head_count = queries.shape[1] // width_per_head
    q_heads = queries.reshape(row_count, head_count, width_per_head).transpose(1, 0, 2)
    k_heads = keys.reshape(row_count, REFL, head_count, width_per_head).transpose(2, 0, 1, 3)
    v_heads = values.reshape(row_count, REFL, head_count, width_per_head).transpose(2, 0, 1, 3)
    b_heads = betas.transpose(2, 0, 1)
    outputs = lax.map(head_pass, (q_heads, k_heads, v_heads, b_heads)).transpose(1, 0, 2)
    normed = outputs * lax.rsqrt(lax.optimization_barrier(jnp.mean(outputs * outputs, axis=-1, keepdims=True)) + epsilon) * norm_gain
    normed = lax.optimization_barrier(normed.astype(jnp.bfloat16))
    gated = normed.astype(jnp.float32).reshape(row_count, head_count * width_per_head) * jax.nn.silu(gate.astype(jnp.float32))
    return gated.astype(jnp.bfloat16)
```

```python
import functools

import jax
import jax.numpy as jnp
from jax import lax
from jax.experimental import pallas as pl
from jax.experimental.pallas import tpu as pltpu
from jax.sharding import Mesh, PartitionSpec as P

EPS = 1e-06
F32 = jnp.float32
BF16 = jnp.bfloat16
PAD = 16
PER_STEP = 2

NN = ((1,), (0,))
NT = ((1,), (1,))
TN = ((0,), (0,))


def dot(a, b, dims=NN):
    return lax.dot_general(a, b, (dims, ((), ())), preferred_element_type=F32)


def split(x):
    hi = x.astype(BF16)
    return hi, (x - hi.astype(F32)).astype(BF16)


def dot3(a, b, dims=NN):
    return dot(a[0], b[0], dims) + (dot(a[0], b[1], dims) + dot(a[1], b[0], dims))


def dot2r(a, b, dims=NN):
    return dot(a, b[0], dims) + dot(a, b[1], dims)


def dot2l(a, b, dims=NN):
    return dot(a[0], b, dims) + dot(a[1], b, dims)


def put(ref, i, parts):
    ref[i, 0] = parts[0]
    ref[i, 1] = parts[1]


def get(ref, i):
    return ref[i, 0], ref[i, 1]


def inverse(grams, g_rows):
    n = grams[0].shape[0]
    row = lax.broadcasted_iota(jnp.int32, (n, n), 0)
    col = lax.broadcasted_iota(jnp.int32, (n, n), 1)
    eye = row == col
    pair = (row // 2 == col // 2) & (row > col)
    out = []
    for gram, g_row in zip(grams, g_rows):
        diag = jnp.where(eye, g_row, 0.0)
        g_col = jnp.sum(diag, axis=1, keepdims=True)
        out.append(diag - jnp.where(pair, g_col * (gram * g_row), 0.0))
    parts = [split(gram) for gram in grams]
    size = 2
    while size < n:
        if size < 8:
            mask = (row // (2 * size) == col // (2 * size)) & (row // size > col // size)
            sp = [split(t) for t in out]
            mid = [split(jnp.where(mask, dot3(t, p), 0.0)) for t, p in zip(sp, parts)]
            out = [t - dot3(m, s) for t, m, s in zip(out, mid, sp)]
        else:
            half = n // 2
            r = lax.broadcasted_iota(jnp.int32, (half, n), 0)
            c = lax.broadcasted_iota(jnp.int32, (half, n), 1)
            mask = c // size == 2 * (r // size)
            cuts = range(0, n, 2 * size)
            odd = [jnp.concatenate([t[i + size : i + 2 * size] for i in cuts], axis=0) for t in out]
            sp = [split(t) for t in out]
            mid = [
                split(jnp.where(mask, dot3(split(o), p), 0.0)) for o, p in zip(odd, parts)
            ]
            low = [o - dot3(m, s) for o, m, s in zip(odd, mid, sp)]
            out = [
                jnp.concatenate(
                    [
                        piece
                        for j, i in enumerate(cuts)
                        for piece in (t[i : i + size], l[j * size : (j + 1) * size])
                    ],
                    axis=0,
                )
                for t, l in zip(out, low)
            ]
        size *= 2
    return out


def keys_kernel(k_ref, ty_ref, w_ref, r_ref, xa_ref, fin_ref, state):
    per, steps, width = k_ref.shape
    steps -= PAD

    @pl.when(pl.program_id(0) == 0)
    def _():
        a = lax.broadcasted_iota(jnp.int32, (width, width), 0)
        b = lax.broadcasted_iota(jnp.int32, (width, width), 1)
        state[...] = jnp.where(a == b, 1.0, 0.0)

    row = lax.broadcasted_iota(jnp.int32, (steps, steps), 0)
    col = lax.broadcasted_iota(jnp.int32, (steps, steps), 1)
    ks = [k_ref[i, :steps] for i in range(per)]
    grams = [dot(k, k, NT) for k in ks]
    sq = [jnp.sum(jnp.where(row == col, g, 0.0), axis=0, keepdims=True) + EPS for g in grams]
    g_rows = [
        k_ref[i, steps : steps + PAD].astype(F32)[0:1] / s for i, s in enumerate(sq)
    ]
    inv = inverse(grams, g_rows)
    for i in range(per):
        put(ty_ref, i, split(inv[i] * jnp.sqrt(sq[i])))
    ws = [split(dot2l(split(t), k)) for t, k in zip(inv, ks)]
    rs = [split(dot2r(k, w, TN)) for k, w in zip(ks, ws)]
    x = state[...]
    for i in range(per):
        put(w_ref, i, ws[i])
        put(r_ref, i, rs[i])
        parts = split(x)
        put(xa_ref, i, parts)
        x = x - dot3(rs[i], parts)
    state[...] = x
    fin_ref[...] = x


def values_kernel(k_ref, v_ref, ty_ref, r_ref, y_ref, xb_ref, fin_ref, state):
    per, steps, width = v_ref.shape

    @pl.when(pl.program_id(0) == 0)
    def _():
        state[...] = jnp.zeros_like(state)

    ys = [split(dot2l(get(ty_ref, i), v_ref[i])) for i in range(per)]
    bs = [dot2r(k_ref[i, :steps], ys[i], TN) for i in range(per)]
    x = state[...]
    for i in range(per):
        put(y_ref, i, ys[i])
        parts = split(x)
        put(xb_ref, i, parts)
        x = x + (bs[i] - dot3(get(r_ref, i), parts))
    state[...] = x
    fin_ref[...] = x


def queries_kernel(q_ref, k_ref, w_ref, y_ref, xa_ref, xb_ref, o_ref, qt_ref):
    per, toks, width = q_ref.shape
    steps = w_ref.shape[2]
    refl = steps // toks
    tok = lax.broadcasted_iota(jnp.int32, (toks, steps), 0)
    step = lax.broadcasted_iota(jnp.int32, (toks, steps), 1)
    causal = step // refl <= tok
    for i in range(per):
        q = q_ref[i]
        qf = q.astype(F32)
        inv = 1.0 / jnp.sqrt(jnp.sum(qf * qf, axis=1, keepdims=True) + EPS)
        s = split(jnp.where(causal, dot(q, k_ref[i, :steps], NT), 0.0))
        qw = split(qf - dot3(s, get(w_ref, i)))
        o_ref[i] = inv * (dot3(qw, get(xb_ref, i)) + dot3(s, get(y_ref, i)))
        qt_ref[i] = inv * dot3(qw, get(xa_ref, i))


def finish_kernel(o_ref, qt_ref, s_ref, gain_ref, out_ref):
    per = o_ref.shape[0]
    s = split(s_ref[...])
    for i in range(per):
        o = o_ref[i] + dot3(split(qt_ref[i]), s)
        mean = jnp.mean(o * o, axis=1, keepdims=True)
        out_ref[i] = (o * lax.rsqrt(mean + EPS) * gain_ref[...]).astype(BF16)


def gate_kernel(n_ref, gate_ref, out_ref):
    per, toks, width = n_ref.shape
    for i in range(per):
        g = gate_ref[:, i * width : (i + 1) * width].astype(F32)
        out_ref[:, i * width : (i + 1) * width] = (
            n_ref[i].astype(F32) * (g / (1.0 + jnp.exp(-g)))
        ).astype(BF16)


def call(kernel, grid, ins, outs, scratch=(), name=None):
    def spec(a, per):
        if per is None:
            return pl.BlockSpec(a.shape, lambda c: (0,) * len(a.shape))
        return pl.BlockSpec((per,) + a.shape[1:], lambda c: (c,) + (0,) * (len(a.shape) - 1))

    return pl.pallas_call(
        kernel,
        grid=(grid,),
        in_specs=[spec(*i) for i in ins],
        out_specs=[spec(*o) for o in outs],
        out_shape=[o[0] for o in outs],
        scratch_shapes=list(scratch),
        name=name,
        compiler_params=pltpu.CompilerParams(dimension_semantics=("arbitrary",)),
    )(*[i[0] for i in ins])


def shards(queries, keys, values, betas, gate, norm_gain):
    toks = queries.shape[0]
    refl = keys.shape[1]
    width = norm_gain.shape[0]
    heads = queries.shape[1] // width
    steps = toks * refl
    near = ("near", "head")
    far_size = lax.axis_size("far")
    group = lax.axis_size("near") * lax.axis_size("head")
    own = heads // group

    def by_head(x, rows):
        return x.reshape(rows, heads, width).transpose(1, 0, 2)

    def exchange(x):
        return lax.all_to_all(x, near, 0, 0, tiled=True)

    b_rows = jnp.broadcast_to(betas.reshape(steps, heads).T[:, None, :], (heads, PAD, steps))
    k = exchange(jnp.concatenate([by_head(keys, steps), b_rows], axis=1))
    v = exchange(by_head(values, steps))
    q = exchange(by_head(queries, toks))

    blocks = group
    per = PER_STEP
    grid = blocks // per
    sds = jax.ShapeDtypeStruct
    pair = sds((blocks, 2, width, width), BF16)
    rows = sds((blocks, 2, steps, width), BF16)
    state = sds((width, width), F32)
    scratch = (pltpu.VMEM((width, width), F32),)
    ty, w, r, xa, end_a = call(
        keys_kernel,
        grid,
        [(k, per)],
        [
            (sds((blocks, 2, steps, steps), BF16), per),
            (rows, per),
            (pair, per),
            (pair, per),
            (state, None),
        ],
        scratch,
        "keys",
    )
    y, xb, end_b = call(
        values_kernel,
        grid,
        [(k, per), (v, per), (ty, per), (r, per)],
        [(rows, per), (pair, per), (state, None)],
        scratch,
        "values",
    )
    route = [(i, i + 1) for i in range(far_size - 1)]
    start = lax.ppermute(end_b, "far", route)
    for _ in range(far_size - 2):
        sent = jnp.dot(end_a, start, precision=lax.Precision.HIGHEST) + end_b
        start = lax.ppermute(sent, "far", route)
    toks_out = sds((blocks, toks, width), F32)
    o, qt = call(
        queries_kernel,
        grid,
        [(q, per), (k, per), (w, per), (y, per), (xa, per), (xb, per)],
        [(toks_out, per), (toks_out, per)],
        (),
        "queries",
    )
    (normed,) = call(
        finish_kernel,
        grid,
        [(o, per), (qt, per), (start, None), (norm_gain[None, :], None)],
        [(sds((blocks, toks, width), BF16), per)],
        (),
        "finish",
    )
    normed = exchange(normed)
    wide = 4
    return pl.pallas_call(
        gate_kernel,
        grid=(heads // wide,),
        in_specs=[
            pl.BlockSpec((wide, toks, width), lambda c: (c, 0, 0)),
            pl.BlockSpec((toks, wide * width), lambda c: (0, c)),
        ],
        out_specs=pl.BlockSpec((toks, wide * width), lambda c: (0, c)),
        out_shape=sds((toks, heads * width), BF16),
        name="gate",
        compiler_params=pltpu.CompilerParams(dimension_semantics=("arbitrary",)),
    )(normed, gate)


def solution(mesh):
    def step(queries, keys, values, betas, gate, norm_gain):
        heads = queries.shape[1] // norm_gain.shape[0]
        seq, head = mesh.shape["seq"], mesh.shape["head"]
        near = heads // head
        fine = Mesh(mesh.devices.reshape(seq // near, near, head), ("far", "near", "head"))
        lead = ("far", "near", "head")
        placed = (
            P(lead, None),
            P(lead, None, None),
            P(lead, None, None),
            P(lead, None, None),
            P(lead, None),
            P(),
        )
        return jax.shard_map(
            shards, mesh=fine, in_specs=placed, out_specs=P(lead, None), check_vma=False
        )(queries, keys, values, betas, gate, norm_gain)

    return step
```

```python
import jax
import jax.numpy as jnp
from jax import lax
from jax.experimental import pallas as pl
from jax.experimental.pallas import tpu as pltpu
from jax.sharding import Mesh, PartitionSpec as P

EPS = 1e-06
F32 = jnp.float32
BF16 = jnp.bfloat16
PAD = 8
LANES = 128
PER_STEP = 4
VMEM_LIMIT = 40 << 20

NN = ((1,), (0,))
NT = ((1,), (1,))
TN = ((0,), (0,))


def dot(a, b, dims=NN):
    return lax.dot_general(a, b, (dims, ((), ())), preferred_element_type=F32)


def split(x):
    hi = x.astype(BF16)
    return hi, (x - hi.astype(F32)).astype(BF16)


def stack(parts, dims):
    axis = 1 - dims[0][0]
    return jnp.concatenate(parts, axis=axis), parts[0].shape[axis]


def dot3(a, b, dims=NN):
    both, rows = stack(a, dims)
    top = dot(both, b[0], dims)
    return top[:rows] + top[rows:] + dot(a[0], b[1], dims)


def dot2r(a, b, dims=NN):
    return dot(a, b[0], dims) + dot(a, b[1], dims)


def dot2l(a, b, dims=NN):
    both, rows = stack(a, dims)
    top = dot(both, b, dims)
    return top[:rows] + top[rows:]


def put(ref, i, parts):
    ref[i, 0] = parts[0]
    ref[i, 1] = parts[1]


def get(ref, i):
    return ref[i, 0], ref[i, 1]


def interleave(even, odd, size):
    pieces = []
    for i in range(0, even.shape[0], size):
        pieces += [even[i : i + size], odd[i : i + size]]
    return jnp.concatenate(pieces, axis=0)


def take(x, size, start):
    return jnp.concatenate(
        [x[i : i + size] for i in range(start, x.shape[0], 2 * size)], axis=0
    )


def block_inverses(grams, g_rows):
    n = grams[0].shape[0]
    row = lax.broadcasted_iota(jnp.int32, (n, n), 0)
    col = lax.broadcasted_iota(jnp.int32, (n, n), 1)
    pair = (row // 2 == col // 2) & (row > col)
    out = []
    for gram, g_row in zip(grams, g_rows):
        diag = jnp.where(row == col, g_row, 0.0)
        g_col = jnp.sum(diag, axis=1, keepdims=True)
        out.append(diag - jnp.where(pair, g_col * (gram * g_row), 0.0))
    parts = [split(gram) for gram in grams]
    size = 2
    while size < n:
        sp = [split(t) for t in out]
        if size < 8:
            mask = (row // (2 * size) == col // (2 * size)) & (row // size > col // size)
            mid = [split(jnp.where(mask, dot3(t, p), 0.0)) for t, p in zip(sp, parts)]
            out = [t - dot3(m, s) for t, m, s in zip(out, mid, sp)]
        else:
            r = lax.broadcasted_iota(jnp.int32, (n // 2, n), 0)
            c = lax.broadcasted_iota(jnp.int32, (n // 2, n), 1)
            mask = c // size == 2 * (r // size)
            odd = [take(t, size, size) for t in out]
            mid = [split(jnp.where(mask, dot3(split(o), p), 0.0)) for o, p in zip(odd, parts)]
            low = [o - dot3(m, s) for o, m, s in zip(odd, mid, sp)]
            out = [interleave(take(t, size, 0), l, size) for t, l in zip(out, low)]
        size *= 2
    return out


def inverses(grams, g_rows):
    n = grams[0].shape[0]
    if n <= LANES:
        return block_inverses(grams, g_rows)
    h = n // 2
    both = inverses(
        [g[:h, :h] for g in grams] + [g[h:, h:] for g in grams],
        [g[:, :h] for g in g_rows] + [g[:, h:] for g in g_rows],
    )
    out = []
    for gram, t1, t2 in zip(grams, both[: len(grams)], both[len(grams) :]):
        mid = dot3(split(gram[h:, :h]), split(t1))
        low = -dot3(split(t2), split(mid))
        out.append(
            jnp.concatenate(
                [
                    jnp.concatenate([t1, jnp.zeros_like(t1)], axis=1),
                    jnp.concatenate([low, t2], axis=1),
                ],
                axis=0,
            )
        )
    return out


def eye(n):
    row = lax.broadcasted_iota(jnp.int32, (n, n), 0)
    return row == lax.broadcasted_iota(jnp.int32, (n, n), 1)


def keys_kernel(k_ref, t_ref, n_ref, rt_ref, e_ref, fin_ref, state):
    per, _, steps, width = t_ref.shape

    @pl.when(pl.program_id(0) == 0)
    def _():
        state[...] = jnp.where(eye(width), 1.0, 0.0)

    diag = eye(steps)
    ks = [k_ref[i, :steps] for i in range(per)]
    grams = [dot(k, k, NT) for k in ks]
    squares = [jnp.where(diag, g, 0.0) for g in grams]
    sq = [jnp.sum(s, axis=0, keepdims=True) + EPS for s in squares]
    n_cols = [jnp.sqrt(jnp.sum(s, axis=1, keepdims=True) + EPS) for s in squares]
    g_rows = [k_ref[i, steps:].astype(F32)[0:1] / s for i, s in enumerate(sq)]
    ts = [split(t) for t in inverses(grams, g_rows)]
    ws = [split(dot2l(t, k)) for t, k in zip(ts, ks)]
    rts = [split(dot2l(w, k, TN)) for k, w in zip(ks, ws)]
    for i in range(per):
        put(t_ref, i, ts[i])
        n_ref[i] = jnp.broadcast_to(jnp.sqrt(sq[i]), n_ref.shape[1:])
        put(rt_ref, i, rts[i])
    f = state[...]
    for i in reversed(range(per)):
        parts = split(f)
        f = f - dot3(rts[i], parts)
        e = dot3(ts[i], split(dot2r(ks[i], parts)), TN)
        put(e_ref, i, split(n_cols[i] * e))
    state[...] = f
    fin_ref[...] = f


def ends_kernel(v_ref, e_ref, fin_ref):
    per = v_ref.shape[0]

    @pl.when(pl.program_id(0) == 0)
    def _():
        fin_ref[...] = jnp.zeros_like(fin_ref)

    total = fin_ref[...]
    for i in range(per):
        total = total + dot2r(v_ref[i], get(e_ref, i), TN)
    fin_ref[...] = total


def local_kernel(q_ref, k_ref, v_ref, t_ref, n_ref, rt_ref, o_ref, qt_ref, state_a, state_b):
    per, toks, width = q_ref.shape
    steps = v_ref.shape[1]
    refl = steps // toks

    @pl.when(pl.program_id(0) == 0)
    def _():
        state_a[...] = jnp.where(eye(width), 1.0, 0.0)
        state_b[...] = jnp.zeros_like(state_b)

    tok = lax.broadcasted_iota(jnp.int32, (toks, steps), 0)
    step = lax.broadcasted_iota(jnp.int32, (toks, steps), 1)
    causal = step // refl <= tok
    a, b = state_a[...], state_b[...]
    for i in range(per):
        q, k, v = q_ref[i], k_ref[i, :steps], v_ref[i]
        t, rt, n_row = get(t_ref, i), get(rt_ref, i), n_ref[i, 0:1]
        qf = q.astype(F32)
        inv = 1.0 / jnp.sqrt(jnp.sum(qf * qf, axis=1, keepdims=True) + EPS)
        s = split(jnp.where(causal, dot(q, k, NT), 0.0))
        st = dot3(s, t)
        qw = split(inv * (qf - dot2l(split(st), k)))
        near = dot2l(split(inv * (st * n_row)), v)
        y = split(dot2l(split((t[0].astype(F32) + t[1].astype(F32)) * n_row), v))
        bt = dot2l(y, k, TN)
        pa, pb = split(a), split(b)
        o_ref[i] = near + dot3(qw, pb, NT)
        put(qt_ref, i, split(dot3(qw, pa, NT)))
        a = a - dot3(pa, rt)
        b = b + (bt - dot3(pb, rt))
    state_a[...] = a
    state_b[...] = b


def finish_kernel(o_ref, qt_ref, s_ref, gain_ref, out_ref):
    s = split(s_ref[...])
    for i in range(o_ref.shape[0]):
        o = o_ref[i] + dot3(get(qt_ref, i), s, NT)
        mean = jnp.mean(o * o, axis=1, keepdims=True)
        out_ref[i] = (o * lax.rsqrt(mean + EPS) * gain_ref[...]).astype(BF16)


def gate_kernel(n_ref, gate_ref, out_ref):
    per, _, width = n_ref.shape
    for i in range(per):
        g = gate_ref[:, i * width : (i + 1) * width].astype(F32)
        out_ref[:, i * width : (i + 1) * width] = (
            n_ref[i].astype(F32) * (g / (1.0 + jnp.exp(-g)))
        ).astype(BF16)


def steps_kernel(x_ref, *rest):
    out_ref = rest[-1]
    per = out_ref.shape[0]
    toks, refl, wide = x_ref.shape
    width = wide // per
    steps = toks * refl
    for i in range(per):
        out_ref[i, :steps] = x_ref[:, :, i * width : (i + 1) * width].reshape(steps, width)
        if len(rest) > 1:
            out_ref[i, steps:] = rest[0][i]


def rows_kernel(x_ref, out_ref):
    per, _, width = out_ref.shape
    for i in range(per):
        out_ref[i] = x_ref[:, i * width : (i + 1) * width]


def params():
    return pltpu.CompilerParams(
        dimension_semantics=("arbitrary",), vmem_limit_bytes=VMEM_LIMIT
    )


def call(kernel, grid, ins, outs, scratch=(), backward=False):
    def spec(a, per):
        zeros = (0,) * (len(a.shape) - 1)
        if per is None:
            return pl.BlockSpec(a.shape, lambda c: (0,) + zeros)
        if backward:
            return pl.BlockSpec((per,) + a.shape[1:], lambda c: (grid - 1 - c,) + zeros)
        return pl.BlockSpec((per,) + a.shape[1:], lambda c: (c,) + zeros)

    return pl.pallas_call(
        kernel,
        grid=(grid,),
        in_specs=[spec(*i) for i in ins],
        out_specs=[spec(*o) for o in outs],
        out_shape=[o[0] for o in outs],
        scratch_shapes=list(scratch),
        compiler_params=params(),
    )(*[i[0] for i in ins])


def by_head(x, width, extra=None, per=4):
    heads = x.shape[-1] // width
    lead = x.shape[:-1]
    rows = lead[0] * (lead[1] if len(lead) > 1 else 1)
    total = rows + (extra.shape[1] if extra is not None else 0)
    zeros = (0,) * len(lead)
    specs = [pl.BlockSpec(lead + (per * width,), lambda c: zeros + (c,))]
    args = [x]
    if extra is not None:
        specs.append(pl.BlockSpec((per,) + extra.shape[1:], lambda c: (c, 0, 0)))
        args.append(extra)
    return pl.pallas_call(
        steps_kernel if len(lead) > 1 else rows_kernel,
        grid=(heads // per,),
        in_specs=specs,
        out_specs=pl.BlockSpec((per, total, width), lambda c: (c, 0, 0)),
        out_shape=jax.ShapeDtypeStruct((heads, total, width), x.dtype),
        name="by_head",
        compiler_params=params(),
    )(*args)


def shards(queries, keys, values, betas, gate, norm_gain):
    toks, refl = keys.shape[:2]
    width = norm_gain.shape[0]
    heads = queries.shape[1] // width
    steps = toks * refl
    near = ("near", "head")
    far_size = lax.axis_size("far")
    blocks = lax.axis_size("near") * lax.axis_size("head")

    def exchange(x):
        return lax.all_to_all(x, near, 0, 0, tiled=True)

    b_rows = jnp.broadcast_to(betas.reshape(steps, heads).T[:, None, :], (heads, PAD, steps))
    k = exchange(by_head(keys, width, b_rows))
    v_out, q_out = by_head(values, width), by_head(queries, width, per=8)
    v = exchange(v_out)

    per = PER_STEP
    grid = blocks // per
    sds = jax.ShapeDtypeStruct
    square = sds((blocks, 2, width, width), BF16)
    state = sds((width, width), F32)
    keep = pltpu.VMEM((width, width), F32)
    t, n, rt, e, end_a = call(
        keys_kernel,
        grid,
        [(k, per)],
        [
            (sds((blocks, 2, steps, steps), BF16), per),
            (sds((blocks, 8, steps), F32), per),
            (square, per),
            (sds((blocks, 2, steps, width), BF16), per),
            (state, None),
        ],
        (keep,),
        backward=True,
    )
    q = exchange(q_out)
    (end_b,) = call(ends_kernel, grid, [(v, per), (e, per)], [(state, None)], ())
    route = [(i, i + 1) for i in range(far_size - 1)]
    start = lax.ppermute(end_b, "far", route)
    for _ in range(far_size - 2):
        sent = jnp.dot(start, end_a, precision=lax.Precision.HIGHEST) + end_b
        start = lax.ppermute(sent, "far", route)
    o, qt = call(
        local_kernel,
        grid,
        [(q, per), (k, per), (v, per), (t, per), (n, per), (rt, per)],
        [(sds((blocks, toks, width), F32), per), (sds((blocks, 2, toks, width), BF16), per)],
        (keep, keep),
    )
    (normed,) = call(
        finish_kernel,
        grid,
        [(o, per), (qt, per), (start, None), (norm_gain[None, :], None)],
        [(sds((blocks, toks, width), BF16), per)],
        (),
    )
    normed = exchange(normed)
    wide = 4
    return pl.pallas_call(
        gate_kernel,
        grid=(heads // wide,),
        in_specs=[
            pl.BlockSpec((wide, toks, width), lambda c: (c, 0, 0)),
            pl.BlockSpec((toks, wide * width), lambda c: (0, c)),
        ],
        out_specs=pl.BlockSpec((toks, wide * width), lambda c: (0, c)),
        out_shape=sds((toks, heads * width), BF16),
        name="gate",
        compiler_params=params(),
    )(normed, gate)


def solution(mesh):
    def step(queries, keys, values, betas, gate, norm_gain):
        heads = queries.shape[1] // norm_gain.shape[0]
        seq, head = mesh.shape["seq"], mesh.shape["head"]
        near = heads // head
        fine = Mesh(mesh.devices.reshape(seq // near, near, head), ("far", "near", "head"))
        lead = ("far", "near", "head")
        placed = (
            P(lead, None),
            P(lead, None, None),
            P(lead, None, None),
            P(lead, None, None),
            P(lead, None),
            P(),
        )

        run = jax.shard_map(
            shards, mesh=fine, in_specs=placed, out_specs=P(lead, None), check_vma=False
        )
        return run(queries, keys, values, betas, gate, norm_gain)

    return step
```

```python
import functools

import jax
import jax.numpy as jnp
from jax import lax
from jax.experimental import pallas as pl
from jax.experimental.pallas import tpu as pltpu
from jax.sharding import Mesh, PartitionSpec as P

EPS = 1e-06
F32 = jnp.float32
BF16 = jnp.bfloat16
PAD = 8
LANES = 128
PER_STEP = 4
VMEM_LIMIT = 40 << 20

NN = ((1,), (0,))
NT = ((1,), (1,))
TN = ((0,), (0,))


def dot(a, b, dims=NN):
    return lax.dot_general(a, b, (dims, ((), ())), preferred_element_type=F32)


def split(x):
    hi = x.astype(BF16)
    return hi, (x - hi.astype(F32)).astype(BF16)


def stack(parts, dims):
    axis = 1 - dims[0][0]
    return jnp.concatenate(parts, axis=axis), parts[0].shape[axis]


def dot3(a, b, dims=NN):
    both, rows = stack(a, dims)
    top = dot(both, b[0], dims)
    return top[:rows] + top[rows:] + dot(a[0], b[1], dims)


def dot2r(a, b, dims=NN):
    return dot(a, b[0], dims) + dot(a, b[1], dims)


def dot2l(a, b, dims=NN):
    both, rows = stack(a, dims)
    top = dot(both, b, dims)
    return top[:rows] + top[rows:]


def put(ref, i, parts):
    ref[i, 0] = parts[0]
    ref[i, 1] = parts[1]


def get(ref, i):
    return ref[i, 0], ref[i, 1]


def interleave(even, odd, size):
    pieces = []
    for i in range(0, even.shape[0], size):
        pieces += [even[i : i + size], odd[i : i + size]]
    return jnp.concatenate(pieces, axis=0)


def take(x, size, start):
    return jnp.concatenate(
        [x[i : i + size] for i in range(start, x.shape[0], 2 * size)], axis=0
    )


def block_inverses(grams, g_rows):
    n = grams[0].shape[0]
    row = lax.broadcasted_iota(jnp.int32, (n, n), 0)
    col = lax.broadcasted_iota(jnp.int32, (n, n), 1)
    pair = (row // 2 == col // 2) & (row > col)
    quad = (row // 4 == col // 4) & (row // 2 > col // 2)
    out = []
    for gram, g_row in zip(grams, g_rows):
        diag = jnp.where(row == col, g_row, 0.0)
        g_col = jnp.sum(diag, axis=1, keepdims=True)
        sub = jnp.where(pair, g_col * (gram * g_row), 0.0)
        s_col = jnp.sum(sub, axis=1, keepdims=True)
        s_row = jnp.sum(sub, axis=0, keepdims=True)
        mid = g_col * gram - s_col * pltpu.roll(gram, 1, 0)
        low = mid * g_row - pltpu.roll(mid, n - 1, 1) * s_row
        out.append(diag - sub - jnp.where(quad, low, 0.0))
    parts = [split(gram) for gram in grams]
    size = 4
    while size < n:
        sp = [split(t) for t in out]
        if size < 8:
            mask = (row // (2 * size) == col // (2 * size)) & (row // size > col // size)
            mid = [split(jnp.where(mask, dot3(t, p), 0.0)) for t, p in zip(sp, parts)]
            out = [t - dot3(m, s) for t, m, s in zip(out, mid, sp)]
        else:
            r = lax.broadcasted_iota(jnp.int32, (n // 2, n), 0)
            c = lax.broadcasted_iota(jnp.int32, (n // 2, n), 1)
            mask = c // size == 2 * (r // size)
            odd = [take(t, size, size) for t in out]
            mid = [split(jnp.where(mask, dot3(split(o), p), 0.0)) for o, p in zip(odd, parts)]
            low = [o - dot3(m, s) for o, m, s in zip(odd, mid, sp)]
            out = [interleave(take(t, size, 0), l, size) for t, l in zip(out, low)]
        size *= 2
    return out


def inverses(grams, g_rows):
    n = grams[0].shape[0]
    if n <= LANES:
        return block_inverses(grams, g_rows)
    h = n // 2
    both = inverses(
        [g[:h, :h] for g in grams] + [g[h:, h:] for g in grams],
        [g[:, :h] for g in g_rows] + [g[:, h:] for g in g_rows],
    )
    out = []
    for gram, t1, t2 in zip(grams, both[: len(grams)], both[len(grams) :]):
        mid = dot3(split(gram[h:, :h]), split(t1))
        low = -dot3(split(t2), split(mid))
        out.append(
            jnp.concatenate(
                [
                    jnp.concatenate([t1, jnp.zeros_like(t1)], axis=1),
                    jnp.concatenate([low, t2], axis=1),
                ],
                axis=0,
            )
        )
    return out


def eye(n):
    row = lax.broadcasted_iota(jnp.int32, (n, n), 0)
    return row == lax.broadcasted_iota(jnp.int32, (n, n), 1)


def keys_kernel(k_ref, t_ref, n_ref, r_ref, e_ref, fin_ref, state, k_s, t_s, r_s, n_s):
    per, _, steps, width = t_ref.shape
    now = pl.program_id(0)
    last = pl.num_programs(0) - 1
    slot = now % 2

    @pl.when(now == 0)
    def _():
        state[...] = jnp.where(eye(width), 1.0, 0.0)

    def front():
        diag = eye(steps)
        ks = [k_ref[i, :steps] for i in range(per)]
        grams = [dot(k, k, NT) for k in ks]
        squares = [jnp.where(diag, g, 0.0) for g in grams]
        sq = [jnp.sum(s, axis=0, keepdims=True) + EPS for s in squares]
        g_rows = [k_ref[i, steps:].astype(F32)[0:1] / s for i, s in enumerate(sq)]
        ts = [split(t) for t in inverses(grams, g_rows)]
        ws = [split(dot2l(t, k)) for t, k in zip(ts, ks)]
        rs = [split(dot2r(k, w, TN)) for k, w in zip(ks, ws)]
        for i in range(per):
            n_row = jnp.sqrt(sq[i])
            n_s[slot, i] = n_row
            n_ref[i] = jnp.broadcast_to(n_row, n_ref.shape[1:])
            k_s[slot, i] = ks[i]
            for j in range(2):
                t_s[slot, i, j] = ts[i][j]
                r_s[slot, i, j] = rs[i][j]
            put(t_ref, i, ts[i])
            put(r_ref, i, rs[i])

    def chain():
        f = state[...]
        for i in reversed(range(per)):
            r = r_s[1 - slot, i, 0], r_s[1 - slot, i, 1]
            t = t_s[1 - slot, i, 0], t_s[1 - slot, i, 1]
            parts = split(f)
            f = f - dot3(parts, r)
            e = dot3(split(dot2l(parts, k_s[1 - slot, i], NT)), t)
            put(e_ref, i, split(e * n_s[1 - slot, i]))
        f = jnp.where(now > 0, f, state[...])
        state[...] = f
        fin_ref[...] = f

    @pl.when(now < last)
    def _():
        chain()
        front()

    @pl.when(now == last)
    def _():
        chain()


def ends_kernel(me_ref, e_ref, *refs, per):
    v_out_ref, fin_ref = refs[-2:]
    step = pl.program_id(0)
    within = me_ref[0] % per
    for g in range((len(refs) - 2) // per):

        @pl.when(step == g)
        def _():
            total = None if g == 0 else fin_ref[...]
            for d in range(per):
                c = within ^ d
                v = refs[g * per + d][...]
                v_out_ref[c] = v
                term = dot2l(get(e_ref, c), v)
                total = term if total is None else total + term
            fin_ref[...] = total


def local_kernel(q_ref, k_ref, v_ref, t_ref, n_ref, r_ref, o_ref, qt_ref, state_a, state_b):
    per, toks, width = q_ref.shape
    steps = v_ref.shape[1]
    refl = steps // toks

    @pl.when(pl.program_id(0) == 0)
    def _():
        state_a[...] = jnp.where(eye(width), 1.0, 0.0)
        state_b[...] = jnp.zeros_like(state_b)

    tok = lax.broadcasted_iota(jnp.int32, (toks, steps), 0)
    step = lax.broadcasted_iota(jnp.int32, (toks, steps), 1)
    causal = step // refl <= tok
    a, b = state_a[...], state_b[...]
    for i in range(per):
        q, k, v = q_ref[i], k_ref[i, :steps], v_ref[i]
        t, r, n_row = get(t_ref, i), get(r_ref, i), n_ref[i, 0:1]
        qf = q.astype(F32)
        inv = 1.0 / jnp.sqrt(jnp.sum(qf * qf, axis=1, keepdims=True) + EPS)
        s = split(jnp.where(causal, dot(q, k, NT), 0.0))
        st = dot3(s, t)
        qw = split(inv * (qf - dot2l(split(st), k)))
        near = dot2l(split(inv * (st * n_row)), v)
        ty = split((t[0].astype(F32) + t[1].astype(F32)) * n_row)
        bt = dot2l(split(dot2r(v, ty, ((0,), (1,)))), k)
        pa, pb = split(a), split(b)
        o_ref[i] = near + dot3(qw, pb, NT)
        put(qt_ref, i, split(dot3(qw, pa, NT)))
        a = a - dot3(pa, r, NT)
        b = b + (bt - dot3(pb, r, NT))
    state_a[...] = a
    state_b[...] = b


def finish_kernel(o_ref, qt_ref, s_ref, gain_ref, out_ref):
    s = split(s_ref[...])
    for i in range(o_ref.shape[0]):
        o = o_ref[i] + dot3(get(qt_ref, i), s)
        mean = jnp.mean(o * o, axis=1, keepdims=True)
        out_ref[i] = (o * lax.rsqrt(mean + EPS) * gain_ref[...]).astype(BF16)


def gate_kernel(n_ref, gate_ref, out_ref):
    per, _, width = n_ref.shape
    for i in range(per):
        g = gate_ref[:, i * width : (i + 1) * width].astype(F32)
        out_ref[:, i * width : (i + 1) * width] = (
            n_ref[i].astype(F32) * (g / (1.0 + jnp.exp(-g)))
        ).astype(BF16)


def steps_kernel(x_ref, *rest):
    out_ref = rest[-1]
    per = out_ref.shape[0]
    toks, refl, wide = x_ref.shape
    width = wide // per
    steps = toks * refl
    for i in range(per):
        out_ref[i, :steps] = x_ref[:, :, i * width : (i + 1) * width].reshape(steps, width)
        if len(rest) > 1:
            out_ref[i, steps:] = rest[0][i]


def apart_kernel(me_ref, x_ref, *out_refs):
    steps, width = out_refs[0].shape
    for d, out_ref in enumerate(out_refs):
        at = pl.multiple_of((me_ref[0] ^ d) * width, width)
        out_ref[...] = x_ref[:, :, pl.ds(at, width)].reshape(steps, width)


def rows_kernel(x_ref, out_ref):
    per, _, width = out_ref.shape
    for i in range(per):
        out_ref[i] = x_ref[:, i * width : (i + 1) * width]


def params():
    return pltpu.CompilerParams(
        dimension_semantics=("arbitrary",), vmem_limit_bytes=VMEM_LIMIT
    )


def in_hbm(x):
    return pltpu.with_memory_space_constraint(x, pltpu.HBM)


def call(kernel, grid, ins, outs, scratch=(), name=None, hbm=True):
    def spec(a, per):
        zeros = (0,) * (len(a.shape) - 1)
        if per is None:
            return pl.BlockSpec(a.shape, lambda c: (0,) + zeros)
        return pl.BlockSpec((per,) + a.shape[1:], lambda c: (c,) + zeros)

    return pl.pallas_call(
        kernel,
        grid=(grid,),
        in_specs=[spec(*i) for i in ins],
        out_specs=[spec(*o) for o in outs],
        out_shape=[
            pltpu.HBM(a.shape, a.dtype) if hbm and per else a for a, per in outs
        ],
        scratch_shapes=list(scratch),
        compiler_params=params(),
    )(*[in_hbm(a) if name == "local" else a for a, _ in ins])


def by_head(x, width, extra=None, per=4):
    heads = x.shape[-1] // width
    lead = x.shape[:-1]
    rows = lead[0] * (lead[1] if len(lead) > 1 else 1)
    total = rows + (extra.shape[1] if extra is not None else 0)
    zeros = (0,) * len(lead)
    specs = [pl.BlockSpec(lead + (per * width,), lambda c: zeros + (c,))]
    args = [x]
    if extra is not None:
        specs.append(pl.BlockSpec((per,) + extra.shape[1:], lambda c: (c, 0, 0)))
        args.append(extra)
    return pl.pallas_call(
        steps_kernel if len(lead) > 1 else rows_kernel,
        grid=(heads // per,),
        in_specs=specs,
        out_specs=pl.BlockSpec((per, total, width), lambda c: (c, 0, 0)),
        out_shape=jax.ShapeDtypeStruct((heads, total, width), x.dtype),
        name="by_head",
        compiler_params=params(),
    )(*args)


SCALAR = pl.BlockSpec(memory_space=pltpu.SMEM)
WHOLE = pl.BlockSpec(memory_space=pltpu.VMEM)


def apart(x, me, count, width):
    steps = x.shape[0] * x.shape[1]
    return pl.pallas_call(
        apart_kernel,
        in_specs=[SCALAR, WHOLE],
        out_specs=[WHOLE] * count,
        out_shape=[jax.ShapeDtypeStruct((steps, width), x.dtype)] * count,
        name="apart",
        compiler_params=pltpu.CompilerParams(vmem_limit_bytes=VMEM_LIMIT),
    )(me, x)


def keys_call(k, blocks, steps, width, per):
    groups = blocks // per
    hbm = [
        ((blocks, 2, steps, steps), BF16),
        ((blocks, 8, steps), F32),
        ((blocks, 2, width, width), BF16),
        ((blocks, 2, width, steps), BF16),
    ]

    def spec(shape, late=0):
        def at(c):
            return (jnp.clip(groups - 1 + late - c, 0, groups - 1),) + (0,) * (len(shape) - 1)

        return pl.BlockSpec((per,) + tuple(shape[1:]), at)

    vmem = pltpu.VMEM
    return pl.pallas_call(
        keys_kernel,
        grid=(groups + 1,),
        in_specs=[spec(k.shape)],
        out_specs=[spec(s, i == 3) for i, (s, _) in enumerate(hbm)]
        + [pl.BlockSpec((width, width), lambda c: (0, 0))],
        out_shape=[pltpu.HBM(*h) for h in hbm] + [jax.ShapeDtypeStruct((width, width), F32)],
        scratch_shapes=[
            vmem((width, width), F32),
            vmem((2, per, steps, width), BF16),
            vmem((2, per, 2, steps, steps), BF16),
            vmem((2, per, 2, width, width), BF16),
            vmem((2, per, 1, steps), F32),
        ],
        name="keys",
        compiler_params=params(),
    )(k)


def ends(me, e, vs, per):
    steps, width = vs[0].shape
    sds = jax.ShapeDtypeStruct

    def at(g, me):
        return (me[0] // per) ^ g

    return pl.pallas_call(
        functools.partial(ends_kernel, per=per),
        grid_spec=pltpu.PrefetchScalarGridSpec(
            num_scalar_prefetch=1,
            grid=(len(vs) // per,),
            in_specs=[pl.BlockSpec((per,) + e.shape[1:], lambda g, me: (at(g, me), 0, 0, 0))]
            + [WHOLE] * len(vs),
            out_specs=[
                pl.BlockSpec((per, steps, width), lambda g, me: (at(g, me), 0, 0)),
                pl.BlockSpec((width, width), lambda g, me: (0, 0)),
            ],
        ),
        out_shape=[pltpu.HBM((len(vs), steps, width), BF16), sds((width, width), F32)],
        name="ends",
        compiler_params=params(),
    )(me, in_hbm(e), *vs)


def shards(queries, keys, values, betas, gate, norm_gain):
    toks, refl = keys.shape[:2]
    width = norm_gain.shape[0]
    heads = queries.shape[1] // width
    steps = toks * refl
    near = ("near", "head")
    far_size = lax.axis_size("far")
    blocks = lax.axis_size("near") * lax.axis_size("head")

    def exchange(x):
        return lax.all_to_all(x, near, 0, 0, tiled=True)

    b_rows = jnp.broadcast_to(betas.reshape(steps, heads).T[:, None, :], (heads, PAD, steps))
    k = exchange(by_head(keys, width, b_rows))
    me = lax.axis_index(near)[None].astype(jnp.int32)
    v_parts = apart(values, me, blocks, width)
    q_out = by_head(queries, width, per=8)
    vs = [v_parts[0]] + [
        lax.ppermute(v_parts[d], near, [(i, i ^ d) for i in range(blocks)])
        for d in range(1, blocks)
    ]

    per = PER_STEP
    grid = blocks // per
    sds = jax.ShapeDtypeStruct
    keep = pltpu.VMEM((width, width), F32)
    t, n, r, e, end_a = keys_call(k, blocks, steps, width, per)
    q = exchange(q_out)
    v, end_b = ends(me, e, vs, per)
    route = [(i, i + 1) for i in range(far_size - 1)]
    start = lax.ppermute(end_b, "far", route)
    for _ in range(far_size - 2):
        sent = jnp.dot(end_a, start, precision=lax.Precision.HIGHEST) + end_b
        start = lax.ppermute(sent, "far", route)
    o, qt = call(
        local_kernel,
        grid,
        [(q, per), (k, per), (v, per), (t, per), (n, per), (r, per)],
        [(sds((blocks, toks, width), F32), per), (sds((blocks, 2, toks, width), BF16), per)],
        (keep, keep),
        "local",
        hbm=False,
    )
    (normed,) = call(
        finish_kernel,
        grid,
        [(o, per), (qt, per), (start, None), (norm_gain[None, :], None)],
        [(sds((blocks, toks, width), BF16), per)],
        (),
        "finish",
        hbm=False,
    )
    normed = exchange(normed)
    wide = 4
    return pl.pallas_call(
        gate_kernel,
        grid=(heads // wide,),
        in_specs=[
            pl.BlockSpec((wide, toks, width), lambda c: (c, 0, 0)),
            pl.BlockSpec((toks, wide * width), lambda c: (0, c)),
        ],
        out_specs=pl.BlockSpec((toks, wide * width), lambda c: (0, c)),
        out_shape=sds((toks, heads * width), BF16),
        name="gate",
        compiler_params=params(),
    )(normed, gate)


def solution(mesh):
    def step(queries, keys, values, betas, gate, norm_gain):
        heads = queries.shape[1] // norm_gain.shape[0]
        seq, head = mesh.shape["seq"], mesh.shape["head"]
        near = heads // head
        fine = Mesh(mesh.devices.reshape(seq // near, near, head), ("far", "near", "head"))
        lead = ("far", "near", "head")
        placed = (
            P(lead, None),
            P(lead, None, None),
            P(lead, None, None),
            P(lead, None, None),
            P(lead, None),
            P(),
        )

        run = jax.shard_map(
            shards, mesh=fine, in_specs=placed, out_specs=P(lead, None), check_vma=False
        )
        return run(queries, keys, values, betas, gate, norm_gain)

    return step
```
